256 devices in a mesh: mem: 8 (over z_lo, core), lat: 32 (over x, y, z_hi).
Axes of the slice: x: 4, y: 4, z: 8 (z_hi: 2, z_lo: 4; z = z_hi * 4 + z_lo), core: 2. Of those that a mesh axis runs over, the one named last changes fastest.
Arguments:
- members: bfloat16 [32, 4, 16, 256, 1024], P('mem', None, None, 'lat'), may hold values from -6 to 6
- increment: float32 [4, 16, 256, 1024], P(None, 'mem', 'lat'), may hold values from -6 to 6
- vertical: float32 [16, 16], replicated, may hold values from -1.5 to 1.5
- lat_taps: float32 [9], replicated, may hold values from 0.2 to 0.6
- lon_taps: float32 [9], replicated, may hold values from 0.2 to 0.6
Outputs:
- product: float32 [4, 16, 256, 1024], P(None, 'mem', 'lat')
The draws below stay inside these ranges and needn't reach their ends.
All inputs are finite; a program needn't handle non-finite values.
Results may differ from the reference program's by a relative error of at most 0.0003.
Values sent between devices are 32-bit elements; how exact they have to be, the bound alone decides.
No kernel may reach another device: no remote copies, remote signals or barrier semaphores. Data moves between devices by JAX's collectives and lax.ppermute only.
A program may use at most 64 MiB of HBM per device.

```python
import jax
import jax.numpy as jnp
from jax import lax

VARS = 4
LEV = 16
TAPS = 9
LON = 1024
MEMBERS = 32
LAT = 256


def shard_levels(rng, extent, pieces, least, high):
    factor_of, own = 1.0, jax.random.fold_in(rng, 6)
    for position, shards_of in pieces:
        heights = jnp.exp(jax.random.uniform(jax.random.fold_in(own, position), (shards_of,), jnp.float32, least / len(pieces), high / len(pieces)))
        factor_of = factor_of * jnp.repeat(heights, extent[position] // shards_of).reshape([-1 if axis == position else 1 for axis in range(len(extent))])
    return factor_of


def gaussian(stream_key, extent, width, reach, pieces=(), held_as=jnp.bfloat16):
    entries = jax.random.normal(stream_key, extent, jnp.float32) * width
    if len(pieces) > 0:
        entries = shard_levels(stream_key, extent, pieces, -0.22, 0.18) * entries
    return jnp.clip(entries, min=-reach, max=reach).astype(held_as)


def setup_inputs(seed: int = 0) -> dict:
    arg_keys = jax.random.split(jax.random.key(seed), 6)
    members = gaussian(arg_keys[0], (MEMBERS, VARS, LEV, LAT, LON), 1.0, 6.0, ((0, 8), (3, 32)))
    increment = gaussian(arg_keys[1], (VARS, LEV, LAT, LON), 1.0, 6.0, ((1, 8), (2, 32)), jnp.float32)
    vertical = gaussian(arg_keys[2], (LEV, LEV), LEV ** -0.5, 1.5, (), jnp.float32)
    lat_taps = jnp.clip(jax.random.uniform(arg_keys[3], (TAPS,), jnp.float32, 0.2, 0.6), 0.2, 0.6)
    lon_taps = jnp.clip(jax.random.uniform(arg_keys[4], (TAPS,), jnp.float32, 0.2, 0.6), 0.2, 0.6)
    return {"members": members, "increment": increment, "vertical": vertical, "lat_taps": lat_taps, "lon_taps": lon_taps}


def lon_adjoint(source, kernel):
    summed = jnp.zeros(source.shape, jnp.float32)
    for offset in range(9):
        summed = summed + kernel[offset] * jnp.roll(source, offset - 4, axis=-1)
    return summed


def lon_forward(source, kernel):
    summed = jnp.zeros(source.shape, jnp.float32)
    for offset in range(9):
        summed = summed + kernel[offset] * jnp.roll(source, 4 - offset, axis=-1)
    return summed


def lat_adjoint(padded, kernel):
    row_count = padded.shape[-2] - 8
    summed = kernel[0] * padded[..., 8:8 + row_count, :]
    for offset in range(1, 9):
        summed = summed + kernel[offset] * padded[..., 8 - offset:8 - offset + row_count, :]
    return summed


def lat_forward(padded, kernel):
    row_count = padded.shape[-2] - 8
    summed = kernel[0] * padded[..., 0:row_count, :]
    for offset in range(1, 9):
        summed = summed + kernel[offset] * padded[..., offset:offset + row_count, :]
    return summed


def pad_rows(source):
    return jnp.pad(source, ((0, 0), (4, 4), (0, 0)))


def reference(members, increment, vertical, lat_taps, lon_taps):
    def member_step(summed, member):
        values = member.astype(jnp.float32)
        weighted = jnp.sum(values * increment, axis=0)
        weighted = lon_adjoint(weighted, lon_taps)
        weighted = jnp.einsum("kl,kij->lij", vertical, weighted, precision=lax.Precision.HIGHEST)
        adjoint_field = lat_adjoint(pad_rows(weighted), lat_taps)
        spread = lat_forward(pad_rows(adjoint_field), lat_taps)
        spread = lon_forward(spread, lon_taps)
        spread = jnp.einsum("lk,kij->lij", vertical, spread, precision=lax.Precision.HIGHEST)
        return summed + values * spread[None], None

    summed, unused = lax.scan(member_step, jnp.zeros(increment.shape, jnp.float32), members)
    return summed / (MEMBERS - 1)
```

```python
import functools

import jax
import jax.numpy as jnp
from jax import lax
from jax.experimental import pallas as pl
from jax.experimental.pallas import tpu as pltpu
from jax.sharding import PartitionSpec as P


WIDTHS = (384, 384, 256)
STARTS = tuple(sum(WIDTHS[:i]) for i in range(len(WIDTHS)))
LEVELS = 16
ROWS = 8
LON = 1024
VARS = 4
LOCAL = 4
CHIPS = 4
FLAT = LEVELS * ROWS
CHIP_ROWS = FLAT // CHIPS
PAIR = 2 * ROWS
SIDE = 128
BLOCK = 256
WINDOW = BLOCK + 2 * SIDE
HIGHEST = lax.Precision.HIGHEST


def split(value):
    high = value.astype(jnp.bfloat16)
    low = (value - high.astype(jnp.float32)).astype(jnp.bfloat16)
    return high, low


def dot(a, b, precision=None):
    return jnp.dot(a, b, preferred_element_type=jnp.float32, precision=precision)


def iotas(*shape):
    return (
        lax.broadcasted_iota(jnp.int32, shape, 0),
        lax.broadcasted_iota(jnp.int32, shape, 1),
    )


def where_one(mask):
    return jnp.where(mask, jnp.float32(1), jnp.float32(0))


def diagonals(distance, values):
    filled = jnp.zeros(distance.shape, jnp.float32)
    for at, value in values:
        filled = jnp.where(distance == at, value, filled)
    return filled


def prepare_kernel(slabs, place, lat_taps, lon_taps, vertical, band_high, band_low, mix):
    chip, core, slab = place[0], place[1], place[2]
    lon = [lon_taps[i] for i in range(9)]
    lat = [lat_taps[i] for i in range(9)]
    square = []
    for shift in range(9):
        terms = [lon[i] * lon[i + shift] for i in range(9 - shift)]
        square.append(functools.reduce(lambda a, b: a + b, terms))
    row, col = iotas(WINDOW, BLOCK)
    distance = jnp.abs(row - SIDE - col)
    band_high[...], band_low[...] = split(diagonals(distance, list(enumerate(square))))

    row, col = iotas(16, 24)
    adjoint = diagonals(row + 8 - col, list(enumerate(lat)))
    line = slab * ROWS - 4 + row
    adjoint = jnp.where((line >= 0) & (line < slabs * ROWS), adjoint, 0.0)
    row, col = iotas(ROWS, 16)
    forward = diagonals(col - row, list(enumerate(lat)))
    band = dot(forward, adjoint, HIGHEST)

    row, col = iotas(LEVELS, LEVELS)
    step, side = row // 4, (row // 2) % 2
    level = 4 * lax.rem(chip - step + CHIPS, CHIPS) + 2 * lax.rem(core + side, 2) + row % 2
    ordered = dot(where_one(level == col), vertical[...], HIGHEST)
    square = lax.dot_general(
        ordered, ordered, (((1,), (1,)), ((), ())), precision=HIGHEST,
        preferred_element_type=jnp.float32,
    )
    row, col = iotas(FLAT, LEVELS)
    tall = where_one(row // ROWS == col)
    row, col = iotas(LEVELS, 3 * FLAT)
    wide = where_one((col % FLAT) // ROWS == row)
    levels = dot(dot(tall, square, HIGHEST), wide, HIGHEST)
    row, col = iotas(FLAT, ROWS)
    tall = where_one(row % ROWS == col)
    row, col = iotas(24, 3 * FLAT)
    odd = lax.rem(slab, 2)
    which = jnp.where(col < FLAT, 1, jnp.where(col < 2 * FLAT, 2 - 2 * odd, 2 * odd))
    wide = where_one(which * ROWS + col % ROWS == row)
    rows = dot(dot(tall, band, HIGHEST), wide, HIGHEST)
    mix[:FLAT], mix[FLAT:] = split(levels * rows)


def prepare(slabs, place, lat_taps, lon_taps, vertical):
    smem = pl.BlockSpec(memory_space=pltpu.SMEM)
    return pl.pallas_call(
        functools.partial(prepare_kernel, slabs),
        out_shape=[
            jax.ShapeDtypeStruct((WINDOW, BLOCK), jnp.bfloat16),
            jax.ShapeDtypeStruct((WINDOW, BLOCK), jnp.bfloat16),
            jax.ShapeDtypeStruct((2 * FLAT, 3 * FLAT), jnp.bfloat16),
        ],
        in_specs=[smem, smem, smem] + whole(1),
        out_specs=whole(3),
        cost_estimate=pl.CostEstimate(flops=1 << 24, bytes_accessed=1 << 20, transcendentals=0),
        name="prepare",
    )(place, lat_taps, lon_taps, vertical)


def whole(count):
    return [pl.BlockSpec(memory_space=pltpu.VMEM)] * count


def weigh_kernel(steps, starts, place, members, *refs):
    chip, core = place[0], place[1]
    count = len(steps)
    parts, (band_high, band_low) = refs[: 2 * count], refs[2 * count : 2 * count + 2]
    outs, both = refs[2 * count + 2 : -1], refs[-1]
    rows_of_one = count * CHIP_ROWS
    rows = LOCAL * rows_of_one

    def member(m, carry):
        for i, step in enumerate(steps):
            for side in range(2):
                part = parts[2 * i + side]
                level = 4 * lax.rem(chip - step + CHIPS, CHIPS) + 2 * lax.rem(core + side, 2)
                total = members[m, 0, pl.ds(level, 2)].astype(jnp.float32) * part[0]
                for v in range(1, VARS):
                    total += members[m, v, pl.ds(level, 2)].astype(jnp.float32) * part[v]
                first = m * rows_of_one + i * CHIP_ROWS + side * PAIR
                for base, value in zip((0, rows), split(total.reshape(PAIR, LON))):
                    line = pl.ds(pl.multiple_of(base + first, PAIR), PAIR)
                    both[line, SIDE : SIDE + LON] = value
                    both[line, :SIDE] = value[:, LON - SIDE :]
                    both[line, SIDE + LON :] = value[:, :SIDE]
        return carry

    lax.fori_loop(0, LOCAL, member, 0)
    for block in range(LON // BLOCK):
        cols = slice(block * BLOCK, block * BLOCK + WINDOW)
        wide = dot(both[:, cols], band_high[...])
        total = wide[:rows] + wide[rows:] + dot(both[:rows, cols], band_low[...])
        total = total.reshape(LOCAL, rows_of_one, BLOCK)
        for half in range(2):
            where = block * BLOCK + half * SIDE
            out = max(i for i in range(len(starts)) if starts[i] <= where)
            to = where - starts[out]
            outs[out][:, :, to : to + SIDE] = total[:, :, half * SIDE : (half + 1) * SIDE]


def weigh(steps, widths, place, members, parts, band):
    starts = tuple(sum(widths[:i]) for i in range(len(widths)))
    rows = len(steps) * CHIP_ROWS
    return pl.pallas_call(
        functools.partial(weigh_kernel, steps, starts),
        out_shape=[jax.ShapeDtypeStruct((LOCAL, rows, w), jnp.float32) for w in widths],
        in_specs=[pl.BlockSpec(memory_space=pltpu.SMEM)] + whole(3 + len(parts)),
        out_specs=whole(len(widths)),
        scratch_shapes=[pltpu.VMEM((2 * LOCAL * rows, LON + 2 * SIDE), jnp.bfloat16)],
        cost_estimate=pl.CostEstimate(
            flops=len(steps) << 28, bytes_accessed=len(steps) << 21, transcendentals=0
        ),
    )(place, members, *parts, *band)


def spread_kernel(start, width, place, members, *refs):
    near, far = refs[:3], refs[3:6]
    mix, keep, give = refs[6], refs[7 : 7 + CHIPS], refs[7 + CHIPS]
    high_ref, low_ref, spread_ref = refs[8 + CHIPS :]
    cols = slice(start, start + width)

    def member(m, carry):
        for at in range(3):
            lines = slice(at * FLAT, at * FLAT + CHIP_ROWS)
            high_ref[lines], low_ref[lines] = split(near[at][m, :, cols])
            lines = slice(at * FLAT + CHIP_ROWS, (at + 1) * FLAT)
            high_ref[lines], low_ref[lines] = split(far[at][m])
        both = dot(mix[...], high_ref[...])
        spread_ref[m] = both[:FLAT] + both[FLAT:] + dot(mix[:FLAT], low_ref[...])
        return carry

    lax.fori_loop(0, LOCAL, member, 0)
    chip, core = place[0], place[1]
    for step in range(CHIPS):
        to = (CHIPS - step) % CHIPS
        for side in range(2):
            first = step * CHIP_ROWS + side * PAIR
            level = 4 * lax.rem(chip - step + CHIPS, CHIPS) + 2 * lax.rem(core + side, 2)
            out = give.at[to] if side else keep[to]
            for v in range(VARS):
                total = None
                for m in range(LOCAL):
                    rows = spread_ref[m, first : first + PAIR].reshape(2, ROWS, width)
                    term = members[m, v, pl.ds(level, 2), :, cols].astype(jnp.float32) * rows
                    total = term if total is None else total + term
                out[v] = total


def spread_product(start, width, place, members, near, far, mix):
    part = jax.ShapeDtypeStruct((VARS, 2, ROWS, width), jnp.float32)
    return pl.pallas_call(
        functools.partial(spread_kernel, start, width),
        out_shape=[part] * CHIPS + [jax.ShapeDtypeStruct((CHIPS, *part.shape), jnp.float32)],
        in_specs=[pl.BlockSpec(memory_space=pltpu.SMEM)] + whole(8),
        out_specs=whole(CHIPS + 1),
        scratch_shapes=[pltpu.VMEM((3 * FLAT, width), jnp.bfloat16)] * 2
        + [pltpu.VMEM((LOCAL, FLAT, width), jnp.float32)],
        cost_estimate=pl.CostEstimate(
            flops=width << 20, bytes_accessed=width * 12 << 10, transcendentals=0
        ),
    )(place, members, *near, *far, mix)


def fold_kernel(*refs):
    keep, got, outs = refs[:CHIPS], refs[CHIPS], refs[CHIPS + 1 :]
    for to in range(CHIPS):
        outs[to][...] = keep[to][...] + got[to]


def fold(keep, got):
    return pl.pallas_call(
        fold_kernel,
        out_shape=[jax.ShapeDtypeStruct(k.shape, k.dtype) for k in keep],
        in_specs=whole(CHIPS + 1),
        out_specs=whole(CHIPS),
        cost_estimate=pl.CostEstimate(flops=got.size, bytes_accessed=12 * got.size, transcendentals=0),
        name="fold",
    )(*keep, got)


def per_device(members, increment, vertical, lat_taps, lon_taps):
    mem, lat = lax.axis_index("mem"), lax.axis_index("lat")
    slabs = lax.axis_size("lat")
    count = LOCAL * lax.axis_size("mem")
    swap_core = [(i, i ^ 1) for i in range(2 * CHIPS)]
    along = lambda step: [(i, (i + 2 * step) % (2 * CHIPS)) for i in range(2 * CHIPS)]
    swap_lat = [(i, i ^ 1) for i in range(slabs)]
    pass_on = [(i, i + 2) for i in range(0, slabs - 2, 2)] + [(i, i - 2) for i in range(3, slabs, 2)]

    held = [increment] + [lax.ppermute(increment, "mem", along(step)) for step in (1, 2, 3)]
    other = [lax.ppermute(part, "mem", swap_core) for part in held]
    index = jnp.arange(3)
    place = jnp.where(index == 0, mem // 2, jnp.where(index == 1, mem % 2, lat)).astype(jnp.int32)
    *band, mix = prepare(slabs, place, lat_taps, lon_taps, vertical)

    (near,) = weigh((0,), (LON,), place, members, [held[0], other[0]], band)
    near = [near, lax.ppermute(near, "lat", swap_lat)]
    near.append(lax.ppermute(near[1], "lat", pass_on))

    parts = [part[step] for step in (1, 2, 3) for part in (held, other)]
    fields = weigh((1, 2, 3), WIDTHS, place, members, parts, band)
    across = [lax.ppermute(field, "lat", swap_lat) for field in fields]
    finals = []
    for i, (start, width) in enumerate(zip(STARTS, WIDTHS)):
        beyond = lax.ppermute(across[i], "lat", pass_on)
        *keep, give = spread_product(
            start, width, place, members, near, [fields[i], across[i], beyond], mix
        )
        got = lax.ppermute(give, "mem", swap_core)
        both = fold(keep, got)
        final = both[0]
        for step in (1, 2, 3):
            final = final + lax.ppermute(both[step], "mem", along(step))
        finals.append(final)
    return jnp.concatenate(finals, axis=-1) / jnp.float32(count - 1)


def solution(mesh):
    in_specs = (P("mem", None, None, "lat", None), P(None, "mem", "lat", None), P(), P(), P())
    out_specs = P(None, "mem", "lat", None)
    return jax.shard_map(
        per_device, mesh=mesh, in_specs=in_specs, out_specs=out_specs, check_vma=False
    )
```

```python
import functools

import jax
import jax.numpy as jnp
from jax import lax
from jax.experimental import pallas as pl
from jax.experimental.pallas import tpu as pltpu
from jax.sharding import PartitionSpec as P


WIDTHS = (384, 384, 256)
STARTS = tuple(sum(WIDTHS[:i]) for i in range(len(WIDTHS)))
LEVELS = 16
ROWS = 8
LON = 1024
VARS = 4
LOCAL = 4
CHIPS = 4
FLAT = LEVELS * ROWS
CHIP_ROWS = FLAT // CHIPS
PAIR = 2 * ROWS
SIDE = 128
BLOCK = 256
WINDOW = BLOCK + 2 * SIDE
GRANT = 24 << 20
HIGHEST = lax.Precision.HIGHEST


def split(value):
    high = value.astype(jnp.bfloat16)
    low = (value - high.astype(jnp.float32)).astype(jnp.bfloat16)
    return high, low


def dot(a, b, precision=None):
    return jnp.dot(a, b, preferred_element_type=jnp.float32, precision=precision)


def iotas(*shape):
    return (
        lax.broadcasted_iota(jnp.int32, shape, 0),
        lax.broadcasted_iota(jnp.int32, shape, 1),
    )


def where_one(mask):
    return jnp.where(mask, jnp.float32(1), jnp.float32(0))


def diagonals(distance, values):
    filled = jnp.zeros(distance.shape, jnp.float32)
    for at, value in values:
        filled = jnp.where(distance == at, value, filled)
    return filled


def prepare_kernel(slabs, place, lat_taps, lon_taps, vertical, band_high, band_low, mix):
    chip, core, slab = place[0], place[1], place[2]
    lon = [lon_taps[i] for i in range(9)]
    lat = [lat_taps[i] for i in range(9)]
    square = []
    for shift in range(9):
        terms = [lon[i] * lon[i + shift] for i in range(9 - shift)]
        square.append(functools.reduce(lambda a, b: a + b, terms))
    row, col = iotas(WINDOW, BLOCK)
    distance = jnp.abs(row - SIDE - col)
    band_high[...], band_low[...] = split(diagonals(distance, list(enumerate(square))))

    row, col = iotas(16, 24)
    adjoint = diagonals(row + 8 - col, list(enumerate(lat)))
    line = slab * ROWS - 4 + row
    adjoint = jnp.where((line >= 0) & (line < slabs * ROWS), adjoint, 0.0)
    row, col = iotas(ROWS, 16)
    forward = diagonals(col - row, list(enumerate(lat)))
    band = dot(forward, adjoint, HIGHEST)

    row, col = iotas(LEVELS, LEVELS)
    step, side = row // 4, (row // 2) % 2
    level = 4 * lax.rem(chip - step + CHIPS, CHIPS) + 2 * lax.rem(core + side, 2) + row % 2
    ordered = dot(where_one(level == col), vertical[...], HIGHEST)
    square = lax.dot_general(
        ordered, ordered, (((1,), (1,)), ((), ())), precision=HIGHEST,
        preferred_element_type=jnp.float32,
    )
    row, col = iotas(FLAT, LEVELS)
    tall = where_one(row // ROWS == col)
    row, col = iotas(LEVELS, 3 * FLAT)
    wide = where_one((col % FLAT) // ROWS == row)
    levels = dot(dot(tall, square, HIGHEST), wide, HIGHEST)
    row, col = iotas(FLAT, ROWS)
    tall = where_one(row % ROWS == col)
    row, col = iotas(24, 3 * FLAT)
    odd = lax.rem(slab, 2)
    which = jnp.where(col < FLAT, 1, jnp.where(col < 2 * FLAT, 2 - 2 * odd, 2 * odd))
    wide = where_one(which * ROWS + col % ROWS == row)
    rows = dot(dot(tall, band, HIGHEST), wide, HIGHEST)
    mix[:FLAT], mix[FLAT:] = split(levels * rows)


def prepare(slabs, place, lat_taps, lon_taps, vertical):
    smem = pl.BlockSpec(memory_space=pltpu.SMEM)
    return pl.pallas_call(
        functools.partial(prepare_kernel, slabs),
        out_shape=[
            pltpu.VMEM((WINDOW, BLOCK), jnp.bfloat16),
            pltpu.VMEM((WINDOW, BLOCK), jnp.bfloat16),
            pltpu.VMEM((2 * FLAT, 3 * FLAT), jnp.bfloat16),
        ],
        in_specs=[smem, smem, smem] + whole(1),
        out_specs=whole(3),
        compiler_params=pltpu.CompilerParams(vmem_limit_bytes=GRANT),
        cost_estimate=pl.CostEstimate(flops=1 << 24, bytes_accessed=1 << 20, transcendentals=0),
        name="prepare",
    )(place, lat_taps, lon_taps, vertical)


def whole(count):
    return [pl.BlockSpec(memory_space=pltpu.VMEM)] * count


def near_core(*arrays):
    return [pltpu.with_memory_space_constraint(a, pltpu.VMEM) for a in arrays]


def weigh_kernel(steps, starts, place, members, *refs):
    chip, core = place[0], place[1]
    count = len(steps)
    parts, (band_high, band_low) = refs[: 2 * count], refs[2 * count : 2 * count + 2]
    outs, both = refs[2 * count + 2 : -1], refs[-1]
    rows_of_one = count * CHIP_ROWS
    rows = LOCAL * rows_of_one

    def member(m, carry):
        for i, step in enumerate(steps):
            for side in range(2):
                part = parts[2 * i + side]
                level = 4 * lax.rem(chip - step + CHIPS, CHIPS) + 2 * lax.rem(core + side, 2)
                total = members[m, 0, pl.ds(level, 2)].astype(jnp.float32) * part[0]
                for v in range(1, VARS):
                    total += members[m, v, pl.ds(level, 2)].astype(jnp.float32) * part[v]
                first = m * rows_of_one + i * CHIP_ROWS + side * PAIR
                for base, value in zip((0, rows), split(total.reshape(PAIR, LON))):
                    line = pl.ds(pl.multiple_of(base + first, PAIR), PAIR)
                    both[line, SIDE : SIDE + LON] = value
                    both[line, :SIDE] = value[:, LON - SIDE :]
                    both[line, SIDE + LON :] = value[:, :SIDE]
        return carry

    lax.fori_loop(0, LOCAL, member, 0)
    for block in range(LON // BLOCK):
        cols = slice(block * BLOCK, block * BLOCK + WINDOW)
        wide = dot(both[:, cols], band_high[...])
        total = wide[:rows] + wide[rows:] + dot(both[:rows, cols], band_low[...])
        total = total.reshape(LOCAL, rows_of_one, BLOCK)
        for half in range(2):
            where = block * BLOCK + half * SIDE
            out = max(i for i in range(len(starts)) if starts[i] <= where)
            to = where - starts[out]
            outs[out][:, :, to : to + SIDE] = total[:, :, half * SIDE : (half + 1) * SIDE]


def weigh(steps, widths, place, members, parts, band):
    starts = tuple(sum(widths[:i]) for i in range(len(widths)))
    rows = len(steps) * CHIP_ROWS
    return pl.pallas_call(
        functools.partial(weigh_kernel, steps, starts),
        out_shape=[pltpu.VMEM((LOCAL, rows, w), jnp.float32) for w in widths],
        in_specs=[pl.BlockSpec(memory_space=pltpu.SMEM)] + whole(3 + len(parts)),
        out_specs=whole(len(widths)),
        scratch_shapes=[pltpu.VMEM((2 * LOCAL * rows, LON + 2 * SIDE), jnp.bfloat16)],
        compiler_params=pltpu.CompilerParams(vmem_limit_bytes=GRANT),
        cost_estimate=pl.CostEstimate(
            flops=len(steps) << 28, bytes_accessed=len(steps) << 21, transcendentals=0
        ),
    )(place, *near_core(members, *parts, *band))


def spread_kernel(start, width, place, members, *refs):
    near, far = refs[:3], refs[3:6]
    mix, keep, give = refs[6], refs[7 : 7 + CHIPS], refs[7 + CHIPS]
    high_ref, low_ref, spread_ref = refs[8 + CHIPS :]
    cols = slice(start, start + width)

    def member(m, carry):
        for at in range(3):
            lines = slice(at * FLAT, at * FLAT + CHIP_ROWS)
            high_ref[lines], low_ref[lines] = split(near[at][m, :, cols])
            lines = slice(at * FLAT + CHIP_ROWS, (at + 1) * FLAT)
            high_ref[lines], low_ref[lines] = split(far[at][m])
        both = dot(mix[...], high_ref[...])
        spread_ref[m] = both[:FLAT] + both[FLAT:] + dot(mix[:FLAT], low_ref[...])
        return carry

    lax.fori_loop(0, LOCAL, member, 0)
    chip, core = place[0], place[1]
    for step in range(CHIPS):
        to = (CHIPS - step) % CHIPS
        for side in range(2):
            first = step * CHIP_ROWS + side * PAIR
            level = 4 * lax.rem(chip - step + CHIPS, CHIPS) + 2 * lax.rem(core + side, 2)
            out = give.at[to] if side else keep[to]
            for v in range(VARS):
                total = None
                for m in range(LOCAL):
                    rows = spread_ref[m, first : first + PAIR].reshape(2, ROWS, width)
                    term = members[m, v, pl.ds(level, 2), :, cols].astype(jnp.float32) * rows
                    total = term if total is None else total + term
                out[v] = total


def spread_product(start, width, place, members, near, far, mix):
    shape = (VARS, 2, ROWS, width)
    return pl.pallas_call(
        functools.partial(spread_kernel, start, width),
        out_shape=[pltpu.VMEM(shape, jnp.float32)] * CHIPS + [pltpu.VMEM((CHIPS, *shape), jnp.float32)],
        in_specs=[pl.BlockSpec(memory_space=pltpu.SMEM)] + whole(8),
        out_specs=whole(CHIPS + 1),
        scratch_shapes=[pltpu.VMEM((3 * FLAT, width), jnp.bfloat16)] * 2
        + [pltpu.VMEM((LOCAL, FLAT, width), jnp.float32)],
        compiler_params=pltpu.CompilerParams(vmem_limit_bytes=GRANT),
        cost_estimate=pl.CostEstimate(
            flops=width << 20, bytes_accessed=width * 12 << 10, transcendentals=0
        ),
    )(place, *near_core(members, *near, *far, mix))


def fold_kernel(*refs):
    keep, got, outs = refs[:CHIPS], refs[CHIPS], refs[CHIPS + 1 :]
    for to in range(CHIPS):
        outs[to][...] = keep[to][...] + got[to]


def fold(keep, got):
    return pl.pallas_call(
        fold_kernel,
        out_shape=[pltpu.VMEM(k.shape, k.dtype) for k in keep],
        in_specs=whole(CHIPS + 1),
        out_specs=whole(CHIPS),
        compiler_params=pltpu.CompilerParams(vmem_limit_bytes=GRANT),
        cost_estimate=pl.CostEstimate(flops=got.size, bytes_accessed=12 * got.size, transcendentals=0),
        name="fold",
    )(*near_core(*keep, got))


def per_device(members, increment, vertical, lat_taps, lon_taps):
    mem, lat = lax.axis_index("mem"), lax.axis_index("lat")
    slabs = lax.axis_size("lat")
    count = LOCAL * lax.axis_size("mem")
    swap_core = [(i, i ^ 1) for i in range(2 * CHIPS)]
    along = lambda step: [(i, (i + 2 * step) % (2 * CHIPS)) for i in range(2 * CHIPS)]
    swap_lat = [(i, i ^ 1) for i in range(slabs)]
    pass_on = [(i, i + 2) for i in range(0, slabs - 2, 2)] + [(i, i - 2) for i in range(3, slabs, 2)]

    held = [increment] + [lax.ppermute(increment, "mem", along(step)) for step in (1, 2, 3)]
    other = [lax.ppermute(part, "mem", swap_core) for part in held]
    index = jnp.arange(3)
    place = jnp.where(index == 0, mem // 2, jnp.where(index == 1, mem % 2, lat)).astype(jnp.int32)
    *band, mix = prepare(slabs, place, lat_taps, lon_taps, vertical)

    (near,) = weigh((0,), (LON,), place, members, [held[0], other[0]], band)
    near = [near, lax.ppermute(near, "lat", swap_lat)]
    near.append(lax.ppermute(near[1], "lat", pass_on))

    parts = [part[step] for step in (1, 2, 3) for part in (held, other)]
    fields = weigh((1, 2, 3), WIDTHS, place, members, parts, band)
    across = [lax.ppermute(field, "lat", swap_lat) for field in fields]
    finals = []
    for i, (start, width) in enumerate(zip(STARTS, WIDTHS)):
        beyond = lax.ppermute(across[i], "lat", pass_on)
        *keep, give = spread_product(
            start, width, place, members, near, [fields[i], across[i], beyond], mix
        )
        got = lax.ppermute(give, "mem", swap_core)
        both = fold(keep, got)
        final = both[0]
        for step in (1, 2, 3):
            final = final + lax.ppermute(both[step], "mem", along(step))
        finals.append(final)
    return jnp.concatenate(finals, axis=-1) / jnp.float32(count - 1)


def solution(mesh):
    in_specs = (P("mem", None, None, "lat", None), P(None, "mem", "lat", None), P(), P(), P())
    out_specs = P(None, "mem", "lat", None)
    return jax.shard_map(
        per_device, mesh=mesh, in_specs=in_specs, out_specs=out_specs, check_vma=False
    )
```

```python
import functools

import jax
import jax.numpy as jnp
from jax import lax
from jax.experimental import pallas as pl
from jax.experimental.pallas import tpu as pltpu
from jax.sharding import PartitionSpec as P


WIDTHS = (256, 256, 256, 256)
STARTS = tuple(sum(WIDTHS[:i]) for i in range(len(WIDTHS)))
GROUPS = ((0, 1), (2,), (3,))
MODES = ('pair', 'pair', 'direct')
LEVELS = 16
ROWS = 8
LON = 1024
VARS = 4
LOCAL = 4
CHIPS = 4
FLAT = LEVELS * ROWS
CHIP_ROWS = FLAT // CHIPS
PAIR = 2 * ROWS
SIDE = 128
BLOCK = 256
WINDOW = BLOCK + 2 * SIDE
GRANT = 24 << 20
HIGHEST = lax.Precision.HIGHEST


def split(value):
    high = value.astype(jnp.bfloat16)
    low = (value - high.astype(jnp.float32)).astype(jnp.bfloat16)
    return high, low


def dot(a, b, precision=None):
    return jnp.dot(a, b, preferred_element_type=jnp.float32, precision=precision)


def iotas(*shape):
    return (
        lax.broadcasted_iota(jnp.int32, shape, 0),
        lax.broadcasted_iota(jnp.int32, shape, 1),
    )


def where_one(mask):
    return jnp.where(mask, jnp.float32(1), jnp.float32(0))


def diagonals(distance, values):
    filled = jnp.zeros(distance.shape, jnp.float32)
    for at, value in values:
        filled = jnp.where(distance == at, value, filled)
    return filled


def prepare_kernel(slabs, place, lat_taps, lon_taps, vertical, members, band_high, band_low, mix):
    chip, core, slab = place[0], place[1], place[2]
    lon = [lon_taps[i] for i in range(9)]
    lat = [lat_taps[i] for i in range(9)]
    square = []
    for shift in range(9):
        terms = [lon[i] * lon[i + shift] for i in range(9 - shift)]
        square.append(functools.reduce(lambda a, b: a + b, terms))
    row, col = iotas(WINDOW, BLOCK)
    distance = jnp.abs(row - SIDE - col)
    band_high[...], band_low[...] = split(diagonals(distance, list(enumerate(square))))

    row, col = iotas(16, 24)
    adjoint = diagonals(row + 8 - col, list(enumerate(lat)))
    line = slab * ROWS - 4 + row
    adjoint = jnp.where((line >= 0) & (line < slabs * ROWS), adjoint, 0.0)
    row, col = iotas(ROWS, 16)
    forward = diagonals(col - row, list(enumerate(lat)))
    band = dot(forward, adjoint, HIGHEST)

    row, col = iotas(LEVELS, LEVELS)
    step, side = row // 4, (row // 2) % 2
    level = 4 * (chip ^ step) + 2 * (core ^ side) + row % 2
    ordered = dot(where_one(level == col), vertical[...], HIGHEST)
    square = lax.dot_general(
        ordered, ordered, (((1,), (1,)), ((), ())), precision=HIGHEST,
        preferred_element_type=jnp.float32,
    )
    row, col = iotas(FLAT, LEVELS)
    tall = where_one(row // ROWS == col)
    row, col = iotas(LEVELS, 3 * FLAT)
    wide = where_one((col % FLAT) // ROWS == row)
    levels = dot(dot(tall, square, HIGHEST), wide, HIGHEST)
    row, col = iotas(FLAT, ROWS)
    tall = where_one(row % ROWS == col)
    row, col = iotas(24, 3 * FLAT)
    odd = lax.rem(slab, 2)
    which = jnp.where(col < FLAT, 1, jnp.where(col < 2 * FLAT, 2 - 2 * odd, 2 * odd))
    wide = where_one(which * ROWS + col % ROWS == row)
    rows = dot(dot(tall, band, HIGHEST), wide, HIGHEST)
    mix[:FLAT], mix[FLAT:] = split(levels * rows)


def prepare(slabs, place, lat_taps, lon_taps, vertical, members):
    smem = pl.BlockSpec(memory_space=pltpu.SMEM)
    return pl.pallas_call(
        functools.partial(prepare_kernel, slabs),
        out_shape=[
            pltpu.VMEM((WINDOW, BLOCK), jnp.bfloat16),
            pltpu.VMEM((WINDOW, BLOCK), jnp.bfloat16),
            pltpu.VMEM((2 * FLAT, 3 * FLAT), jnp.bfloat16),
        ],
        in_specs=[smem, smem, smem] + whole(2),
        out_specs=whole(3),
        compiler_params=pltpu.CompilerParams(vmem_limit_bytes=GRANT),
        cost_estimate=pl.CostEstimate(flops=1 << 24, bytes_accessed=1 << 20, transcendentals=0),
        name="prepare",
    )(place, lat_taps, lon_taps, *near_core(vertical, members))


def whole(count):
    return [pl.BlockSpec(memory_space=pltpu.VMEM)] * count


def near_core(*arrays):
    return [pltpu.with_memory_space_constraint(a, pltpu.VMEM) for a in arrays]


def weigh_kernel(steps, starts, place, members, *refs):
    chip, core = place[0], place[1]
    count = len(steps)
    parts, (band_high, band_low) = refs[: 2 * count], refs[2 * count : 2 * count + 2]
    outs, both = refs[2 * count + 2 : -1], refs[-1]
    rows_of_one = count * CHIP_ROWS
    rows = LOCAL * rows_of_one

    def member(m, carry):
        for i, step in enumerate(steps):
            for side in range(2):
                part = parts[2 * i + side]
                level = 4 * (chip ^ step) + 2 * (core ^ side)
                total = members[m, 0, pl.ds(level, 2)].astype(jnp.float32) * part[0]
                for v in range(1, VARS):
                    total += members[m, v, pl.ds(level, 2)].astype(jnp.float32) * part[v]
                first = m * rows_of_one + i * CHIP_ROWS + side * PAIR
                for base, value in zip((0, rows), split(total.reshape(PAIR, LON))):
                    line = pl.ds(pl.multiple_of(base + first, PAIR), PAIR)
                    both[line, SIDE : SIDE + LON] = value
                    both[line, :SIDE] = value[:, LON - SIDE :]
                    both[line, SIDE + LON :] = value[:, :SIDE]
        return carry

    lax.fori_loop(0, LOCAL, member, 0)
    for block in range(LON // BLOCK):
        cols = slice(block * BLOCK, block * BLOCK + WINDOW)
        wide = dot(both[:, cols], band_high[...])
        total = wide[:rows] + wide[rows:] + dot(both[:rows, cols], band_low[...])
        total = total.reshape(LOCAL, rows_of_one, BLOCK)
        for half in range(2):
            where = block * BLOCK + half * SIDE
            out = max(i for i in range(len(starts)) if starts[i] <= where)
            to = where - starts[out]
            outs[out][:, :, to : to + SIDE] = total[:, :, half * SIDE : (half + 1) * SIDE]


def weigh(steps, widths, place, members, parts, band):
    starts = tuple(sum(widths[:i]) for i in range(len(widths)))
    rows = len(steps) * CHIP_ROWS
    return pl.pallas_call(
        functools.partial(weigh_kernel, steps, starts),
        out_shape=[pltpu.VMEM((LOCAL, rows, w), jnp.float32) for w in widths],
        in_specs=[pl.BlockSpec(memory_space=pltpu.SMEM)] + whole(3 + len(parts)),
        out_specs=whole(len(widths)),
        scratch_shapes=[pltpu.VMEM((2 * LOCAL * rows, LON + 2 * SIDE), jnp.bfloat16)],
        compiler_params=pltpu.CompilerParams(vmem_limit_bytes=GRANT),
        cost_estimate=pl.CostEstimate(
            flops=len(steps) << 28, bytes_accessed=len(steps) << 21, transcendentals=0
        ),
    )(place, members, *near_core(*parts, *band))


def spread_kernel(start, widths, place, members, mix, *refs):
    near, far = refs[:3], refs[3 : 3 + 3 * len(widths)]
    keep, give, high_ref, low_ref, spread_ref = refs[3 + 3 * len(widths) :]
    width = sum(widths)
    cols = slice(start, start + width)

    def member(m, carry):
        for at in range(3):
            lines = slice(at * FLAT, at * FLAT + CHIP_ROWS)
            high_ref[lines], low_ref[lines] = split(near[at][m, :, cols])
            lines = slice(at * FLAT + CHIP_ROWS, (at + 1) * FLAT)
            for i, w in enumerate(widths):
                to = slice(sum(widths[:i]), sum(widths[:i]) + w)
                high_ref[lines, to], low_ref[lines, to] = split(far[3 * i + at][m])
        both = dot(mix[...], high_ref[...])
        spread_ref[m] = both[:FLAT] + both[FLAT:] + dot(mix[:FLAT], low_ref[...])
        return carry

    lax.fori_loop(0, LOCAL, member, 0)
    chip, core = place[0], place[1]
    for step in range(CHIPS):
        for side in range(2):
            first = step * CHIP_ROWS + side * PAIR
            level = 4 * (chip ^ step) + 2 * (core ^ side)
            out = (give if side else keep).at[step]
            for v in range(VARS):
                total = None
                for m in range(LOCAL):
                    rows = spread_ref[m, first : first + PAIR].reshape(2, ROWS, width)
                    term = members[m, v, pl.ds(level, 2), :, cols].astype(jnp.float32) * rows
                    total = term if total is None else total + term
                out[v] = total


def spread_product(start, widths, place, members, near, far, mix):
    width = sum(widths)
    shape = (CHIPS, VARS, 2, ROWS, width)
    return pl.pallas_call(
        functools.partial(spread_kernel, start, widths),
        out_shape=[pltpu.VMEM(shape, jnp.float32)] * 2,
        in_specs=[pl.BlockSpec(memory_space=pltpu.SMEM)] + whole(5 + len(far)),
        out_specs=whole(2),
        scratch_shapes=[pltpu.VMEM((3 * FLAT, width), jnp.bfloat16)] * 2
        + [pltpu.VMEM((LOCAL, FLAT, width), jnp.float32)],
        compiler_params=pltpu.CompilerParams(vmem_limit_bytes=GRANT),
        cost_estimate=pl.CostEstimate(
            flops=width << 20, bytes_accessed=width * 12 << 10, transcendentals=0
        ),
    )(place, members, *near_core(mix, *near, *far))


def fold_kernel(groups, keep, got, *outs):
    for out, group in zip(outs, groups):
        for to, at in enumerate(group):
            out[to] = keep[at] + got[at]


def fold(keep, got, groups):
    return pl.pallas_call(
        functools.partial(fold_kernel, groups),
        out_shape=[pltpu.VMEM((len(g), *got.shape[1:]), jnp.float32) for g in groups],
        in_specs=whole(2),
        out_specs=whole(len(groups)),
        compiler_params=pltpu.CompilerParams(vmem_limit_bytes=GRANT),
        cost_estimate=pl.CostEstimate(flops=got.size, bytes_accessed=12 * got.size, transcendentals=0),
        name="fold",
    )(*near_core(keep, got))


def move(array, axis, pairs):
    return lax.ppermute(array, axis, pairs)


def per_device(members, increment, vertical, lat_taps, lon_taps):
    mem, lat = lax.axis_index("mem"), lax.axis_index("lat")
    slabs = lax.axis_size("lat")
    count = LOCAL * lax.axis_size("mem")
    swap = lambda bit: [(i, i ^ bit) for i in range(2 * CHIPS)]
    swap_lat = [(i, i ^ 1) for i in range(slabs)]
    pass_on = [(i, i + 2) for i in range(0, slabs - 2, 2)] + [(i, i - 2) for i in range(3, slabs, 2)]

    held = [increment, move(increment, "mem", swap(2)), move(increment, "mem", swap(4))]
    held.append(move(held[2], "mem", swap(2)))
    other = [move(part, "mem", swap(1)) for part in held]
    index = jnp.arange(3)
    place = jnp.where(index == 0, mem // 2, jnp.where(index == 1, mem % 2, lat)).astype(jnp.int32)
    (members,) = near_core(members)
    *band, mix = prepare(slabs, place, lat_taps, lon_taps, vertical, members)

    (near,) = weigh((0,), (LON,), place, members, [held[0], other[0]], band)
    near = [near, move(near, "lat", swap_lat)]
    near.append(move(near[1], "lat", pass_on))

    parts = [part[step] for step in (1, 2, 3) for part in (held, other)]
    fields = weigh((1, 2, 3), WIDTHS, place, members, parts, band)
    across = [move(field, "lat", swap_lat) for field in fields]
    beyond = [move(field, "lat", pass_on) for field in across]
    finals = []
    for i, group in enumerate(GROUPS):
        far = [kind[piece] for piece in group for kind in (fields, across, beyond)]
        widths = [WIDTHS[piece] for piece in group]
        keep, give = spread_product(STARTS[group[0]], widths, place, members, near, far, mix)
        got = move(give, "mem", swap(1))
        if MODES[i] == "pair":
            keep, give = fold(keep, got, ((0, 2), (1, 3)))
            got = move(give, "mem", swap(2))
            keep, give = fold(keep, got, ((0,), (1,)))
            finals.append(keep[0] + move(give, "mem", swap(4))[0])
        else:
            keep, *gives = fold(keep, got, ((0,), (1,), (2,), (3,)))
            final = keep[0]
            for step in (1, 2, 3):
                final = final + move(gives[step - 1], "mem", swap(2 * step))[0]
            finals.append(final)
    return jnp.concatenate(finals, axis=-1) / jnp.float32(count - 1)


def solution(mesh):
    in_specs = (P("mem", None, None, "lat", None), P(None, "mem", "lat", None), P(), P(), P())
    out_specs = P(None, "mem", "lat", None)
    return jax.shard_map(
        per_device, mesh=mesh, in_specs=in_specs, out_specs=out_specs, check_vma=False
    )
```
